32 devices in a mesh: slab: 2 (over y), row: 16 (over z, x, core).
Axes of the slice: x: 2, y: 2, z: 4, core: 2. Of those that a mesh axis runs over, the one named last changes fastest.
Arguments:
- calib: bfloat16 [2048, 8192], P('slab', 'row'), parts along dimension 0, may hold values from -6 to 6
- weights: bfloat16 [16384, 512], P(('slab', 'row')), parts along dimension 0, may hold values from -0.25 to 0.25
- hess_inv: float32 [16384, 8192], P(('slab', 'row')), parts along dimension 0, as said below
- block_scale: float32 [512, 512], P(('slab', 'row')), parts along dimension 0, may hold values from 0.04 to 0.4
Outputs:
- rounded: float32 [16384, 512], P(('slab', 'row')), parts along dimension 0
- dual: float32 [16384, 512], P(('slab', 'row')), parts along dimension 0
The draws below stay inside these ranges and needn't reach their ends.
There are 2 independent parts, one for each index of `slab`. The reference program is written for one: setup_inputs(seed, part) draws one part's arguments, and reference() takes and returns one part's arrays. A program takes and returns all parts, laid end to end along the dimension named above; each array names one. Nothing has to cross between parts.
Inputs may be any that keep to these rules, and one draw needn't show every extreme that they name: hess_inv is symmetric and positive definite.
All inputs are finite; a program needn't handle non-finite values.
Results may differ from the reference program's by a relative error of at most 0.011.
The reference program's roundings to bfloat16 on the way (of `outputs16` and `right`) count: a program that leaves them out, or rounds other values in their place, can miss the bound.
Values may be sent and summed in bfloat16 or wider, within the bound.
No kernel may reach another device: no remote copies, remote signals or barrier semaphores. Data moves between devices by JAX's collectives and lax.ppermute only.
A program may use at most 64 MiB of HBM per device.

```python
import math
import jax
import jax.numpy as jnp
from jax import lax

K = 8192
C = 512
TOKENS = 1024
HB = 32
ITERS = 3


def draw_hess_inv(key, part):
    base = jax.random.fold_in(key, 11)
    first, second = jax.random.split(base)
    noise = jax.random.normal(first, (K, K), jnp.float32)
    middle = jax.random.uniform(second, (K,), jnp.float32, 0.6, 1.2)
    spread = jnp.float32(0.25 / math.sqrt(2.0 * K))
    return jnp.diag(middle) + (noise + noise.T) * spread


def level_of(own_key, dims, pieces, least, largest):
    gain, own = 1.0, jax.random.fold_in(own_key, 6)
    for position, blocks in pieces:
        draws = jnp.exp(jax.random.uniform(jax.random.fold_in(own, position), (blocks,), jnp.float32, least / len(pieces), largest / len(pieces)))
        gain = gain * jnp.repeat(draws, dims[position] // blocks).reshape([-1 if axis == position else 1 for axis in range(len(dims))])
    return gain


def scatter_about(stream_key, dims, deviation, bound, cuts=(), held_as=jnp.bfloat16):
    loudness = level_of(stream_key, dims, cuts, -0.22, 0.18) if cuts else 1.0
    array = jax.random.normal(stream_key, dims, jnp.float32) * deviation * loudness
    return jnp.minimum(jnp.maximum(array, -bound), bound).astype(held_as)


def setup_inputs(seed: int = 0, part: int = 0) -> dict:
    streams_of = jax.random.split(jax.random.key(seed), 5)
    own_keys = jax.random.split(jax.random.fold_in(streams_of[4], part), 5)
    return {
        "calib": scatter_about(own_keys[0], (TOKENS, K), 1.0, 6.0, ((1, 16),)),
        "weights": jnp.clip(jax.random.uniform(own_keys[1], (K, C), jnp.float32, -0.25, 0.25) * level_of(own_keys[1], (K, C), ((0, 16),), -0.4, 0.0), -0.25, 0.25).astype(jnp.bfloat16),
        "hess_inv": draw_hess_inv(jax.random.fold_in(jax.random.fold_in(streams_of[4], part), 71), part),
        "block_scale": jnp.clip(jnp.exp(math.log(0.4) - 2.3025851 * jax.random.uniform(own_keys[3], (K // HB, C), jnp.float32) ** level_of(own_keys[3], (K // HB, C), ((0, 16),), -0.2, 0.2)), 0.04, 0.4),
    }


def hadamard_table(width):
    index = jnp.arange(width, dtype=jnp.int32)
    left = index[:, None]
    right = index[None, :]
    parity = jnp.zeros((width, width), jnp.int32)
    for bit in range(width.bit_length() - 1):
        parity = parity + jnp.bitwise_and(jnp.right_shift(left, bit), 1) * jnp.bitwise_and(jnp.right_shift(right, bit), 1)
    signs = jnp.where(parity % 2 == 0, 1.0, -1.0).astype(jnp.float32)
    return signs * jnp.float32(1.0 / math.sqrt(width))

def blockwise(values, table):
    rows, cols = values.shape
    width = table.shape[0]
    blocks = values.reshape(rows // width, width, cols)
    spun = jnp.einsum('ij,bjc->bic', table, blocks, precision=lax.Precision.HIGHEST)
    return spun.reshape(rows, cols)

def project(solved, dual, scale, table):
    width = table.shape[0]
    rows, cols = solved.shape
    spun = blockwise(solved + dual, table).reshape(rows // width, width, cols)
    shares = scale[:, None, :]
    ratio = spun / shares
    snapped = shares * (ratio - jnp.sin(2.0 * math.pi * ratio) / (4.0 * math.pi))
    return blockwise(snapped.reshape(rows, cols), table)

def reference(calib, weights, hess_inv, block_scale):
    table = hadamard_table(HB)
    outputs = jnp.dot(calib, weights, preferred_element_type=jnp.float32)
    outputs16 = outputs.astype(jnp.bfloat16)
    factor = jnp.float32(0.25 / math.sqrt(K * TOKENS))
    target = lax.dot_general(calib, outputs16, (((0,), (0,)), ((), ())), preferred_element_type=jnp.float32) * factor
    current = weights.astype(jnp.float32)
    dual = jnp.zeros_like(current)
    for step in range(ITERS):
        right = (target + 0.5 * (current - dual)).astype(jnp.bfloat16)
        solved = jnp.dot(hess_inv, right.astype(jnp.float32), precision=lax.Precision.HIGHEST)
        fresh = project(solved, dual, block_scale, table)
        dual = dual + solved - fresh
        current = fresh
    return (current, dual)
```

```python
import math

import jax
import jax.numpy as jnp
from jax import lax
from jax.sharding import PartitionSpec as P

HB = 32
ITERS = 3
F32 = jnp.float32
BF16 = jnp.bfloat16


SINE = (
    6.283185288846474,
    -16.208955714017648,
    16.769156840921543,
    -9.623969670500662,
    3.5124157106410516,
    -0.7904000717077384,
)


def hadamard_signs(width, size):
    index = jnp.arange(size, dtype=jnp.int32)
    left = index[:, None]
    right = index[None, :]
    parity = jnp.zeros((size, size), jnp.int32)
    for bit in range(width.bit_length() - 1):
        parity = parity + jnp.bitwise_and(jnp.right_shift(left, bit), 1) * jnp.bitwise_and(
            jnp.right_shift(right, bit), 1
        )
    signs = jnp.where(parity % 2 == 0, 1.0, -1.0)
    same = (left // width) == (right // width)
    return jnp.where(same, signs, 0.0).astype(BF16)


def split(values):
    high = lax.reduce_precision(values, 8, 7)
    return high.astype(BF16), (values - high).astype(BF16)


def dot(a, b, dims):
    return lax.dot_general(a, b, (dims, ((), ())), preferred_element_type=F32)


def blockwise(values, signs):
    rows, cols = values.shape
    width = signs.shape[0]
    high, low = split(values)
    parts = []
    for at in range(0, rows, width):
        parts.append(
            dot(signs, high[at : at + width], ((1,), (0,)))
            + dot(signs, low[at : at + width], ((1,), (0,)))
        )
    return jnp.concatenate(parts, axis=0)


def sine_turns(t):
    r = t - jnp.round(t)
    square = r * r
    series = F32(SINE[-1])
    for term in SINE[-2::-1]:
        series = series * square + F32(term)
    return (r - 4.0 * square * r) * series


def project(solved, dual, scale, signs):
    rows, cols = solved.shape
    spun = blockwise(solved + dual, signs) * F32(1.0 / math.sqrt(HB))
    spun = spun.reshape(rows // HB, HB, cols)
    shares = scale[:, None, :]
    ratio = spun / shares
    snapped = shares * (ratio - sine_turns(ratio) / (4.0 * math.pi))
    snapped = snapped.reshape(rows, cols)
    return blockwise(snapped, signs) * F32(1.0 / math.sqrt(HB))


class Line:
    def __init__(self, dims, axis):
        self.dims, self.axis, self.n = dims, axis, dims[axis]

    def pairs(self, move, keep=lambda at: True):
        out = []
        z_n, x_n, c_n = self.dims
        for z in range(z_n):
            for x in range(x_n):
                for c in range(c_n):
                    at = [z, x, c]
                    if not keep(at):
                        continue
                    to = list(at)
                    to[self.axis] = move(at[self.axis])
                    if 0 <= to[self.axis] < self.n:
                        flat = [(p[0] * x_n + p[1]) * c_n + p[2] for p in (at, to)]
                        out.append(tuple(flat))
        return out

    def send(self, value, move, keep=lambda at: True):
        return lax.ppermute(value, "row", self.pairs(move, keep))


def make_fast(dims):
    n = dims[0]
    zline, xline, cline = (Line(dims, axis) for axis in range(3))

    def swap_x(value, keep=lambda at: True):
        return xline.send(value, lambda p: 1 - p, keep)

    def swap_c(value):
        return cline.send(value, lambda p: 1 - p)

    def gather(own):
        arrive = {}
        far = {}
        up = down = own
        arrive[0] = own
        far[0] = swap_x(own)
        pieces = []
        for s in range(1, n):
            up = zline.send(up, lambda p: p + 1, lambda at, s=s: at[0] >= s - 1)
            down = zline.send(down, lambda p: p - 1, lambda at, s=s: at[0] <= n - s)
            has_up = lambda at, s=s: at[0] >= s
            has_down = lambda at, s=s: at[0] <= n - 1 - s
            pieces.append((s, up, down, has_up, has_down))
        ups, downs, fups, fdowns = {}, {}, {}, {}
        for s, u, d, hu, hd in pieces:
            ups[s], downs[s] = u, d
            fups[s], fdowns[s] = swap_x(u, hu), swap_x(d, hd)
        near = [own] + [downs[o] + ups[n - o] for o in range(1, n)]
        over = [far[0]] + [fdowns[o] + fups[n - o] for o in range(1, n)]
        near, over = jnp.concatenate(near, axis=0), jnp.concatenate(over, axis=0)
        return ((near, over), (swap_c(near), swap_c(over)))

    def scatter(parts):
        mine = [parts[0][xo] + swap_c(parts[1][xo].astype(BF16)).astype(F32) for xo in range(2)]
        mine = jnp.stack(mine, axis=1)
        up = down = None
        for s in range(1, n):
            u = mine[n - s] if up is None else mine[n - s] + up.astype(F32)
            d = mine[s] if down is None else mine[s] + down.astype(F32)
            up = zline.send(u.astype(BF16), lambda p: p + 1, lambda at, s=s: at[0] <= s - 1)
            down = zline.send(d.astype(BF16), lambda p: p - 1, lambda at, s=s: at[0] >= n - s)
        own = mine[0] + up.astype(F32) + down.astype(F32)
        return own[0] + swap_x(own[1].astype(BF16)).astype(F32)

    def reduce_tokens(partial, z, x, c):
        tokens = partial.shape[0]
        half, quarter = tokens // 2, tokens // 4
        block = quarter // n
        mine = lax.dynamic_slice_in_dim(partial, c * half, half, 0)
        give = lax.dynamic_slice_in_dim(partial, (1 - c) * half, half, 0)
        mine = mine + swap_c(give)
        give = lax.dynamic_slice_in_dim(mine, (1 - x) * quarter, quarter, 0)
        mine = lax.dynamic_slice_in_dim(mine, x * quarter, quarter, 0)
        mine = mine + swap_x(give)
        got = []
        for o in range(1, n):
            give = lax.dynamic_slice_in_dim(mine, ((z + o) % n) * block, block, 0)
            got.append(zline.send(give, lambda p, o=o: (p + o) % n))
        total = lax.dynamic_slice_in_dim(mine, z * block, block, 0)
        for g in got:
            total = total + g
        total = total.astype(BF16)
        full = jnp.zeros((quarter, partial.shape[1]), BF16)
        full = lax.dynamic_update_slice_in_dim(full, total, z * block, 0)
        for o in range(1, n):
            g = zline.send(total, lambda p, o=o: (p + o) % n)
            full = lax.dynamic_update_slice_in_dim(full, g, ((z + n - o) % n) * block, 0)
        other = swap_x(full)
        low = jnp.where(x == 0, full, other)
        high = jnp.where(x == 0, other, full)
        full = jnp.concatenate([low, high], axis=0)
        other = swap_c(full)
        low = jnp.where(c == 0, full, other)
        high = jnp.where(c == 0, other, full)
        return jnp.concatenate([low, high], axis=0)

    def body(calib, weights, hess_inv, block_scale):
        rows, cols = weights.shape
        tokens = calib.shape[0]
        inner = hess_inv.shape[1]
        at = lax.axis_index("row")
        c = at % 2
        x = (at // 2) % 2
        z = at // 4
        signs = hadamard_signs(HB, 256)
        factor = F32(0.25 / math.sqrt(inner * tokens))
        width = cols // 4
        spans = [slice(i * width, (i + 1) * width) for i in range(4)]

        partial = [dot(calib, weights[:, s], ((1,), (0,))) for s in spans]
        outputs = [reduce_tokens(p, z, x, c) for p in partial]

        groups = []
        for co in range(2):
            for xo in range(2):
                blocks = []
                for o in range(n):
                    src = (((z + o) % n) * 2 + jnp.bitwise_xor(x, xo)) * 2 + jnp.bitwise_xor(c, co)
                    blocks.append(
                        lax.dynamic_slice_in_dim(hess_inv, src * rows, rows, 1).astype(BF16)
                    )
                groups.append(jnp.concatenate(blocks, axis=1))
        own_block = lax.dynamic_slice_in_dim(hess_inv, at * rows, rows, 1)
        own_low = split(own_block)[1]

        target = [dot(calib, o, ((0,), (0,))) * factor for o in outputs]
        current = [weights[:, s].astype(F32) for s in spans]
        dual = [jnp.zeros_like(v) for v in current]
        scales = [block_scale[:, s] for s in spans]
        for step in range(ITERS):
            for i in range(4):
                right = (target[i] + 0.5 * (current[i] - dual[i])).astype(BF16)
                if i < 3:
                    got = gather(right)
                    solved = dot(own_low, right, ((1,), (0,)))
                    for co in range(2):
                        for xo in range(2):
                            solved = solved + dot(
                                groups[co * 2 + xo], got[co][xo], ((1,), (0,))
                            )
                else:
                    parts = [
                        [
                            dot(groups[co * 2 + xo], right, ((0,), (0,))).reshape(n, rows, width)
                            for xo in range(2)
                        ]
                        for co in range(2)
                    ]
                    solved = scatter(parts) + dot(own_low, right, ((1,), (0,)))
                fresh = project(solved, dual[i], scales[i], signs)
                dual[i] = dual[i] + solved - fresh
                current[i] = fresh
        return (jnp.concatenate(current, axis=1), jnp.concatenate(dual, axis=1))

    return body


def body_any(calib, weights, hess_inv, block_scale):
    signs = hadamard_signs(HB, math.gcd(weights.shape[0], 256))
    outputs = lax.psum(dot(calib, weights, ((1,), (0,))), "row").astype(BF16)
    factor = F32(0.25 / math.sqrt(hess_inv.shape[1] * calib.shape[0]))
    target = dot(calib, outputs, ((0,), (0,))) * factor
    high, low = split(hess_inv)
    current = weights.astype(F32)
    dual = jnp.zeros_like(current)
    for step in range(ITERS):
        right = (target + 0.5 * (current - dual)).astype(BF16)
        right = lax.all_gather(right, "row", axis=0, tiled=True)
        solved = dot(high, right, ((1,), (0,))) + dot(low, right, ((1,), (0,)))
        fresh = project(solved, dual, block_scale, signs)
        dual = dual + solved - fresh
        current = fresh
    return (current, dual)


def solution(mesh):
    line = mesh.devices.reshape(mesh.shape["slab"], mesh.shape["row"])[0]
    spread = [{d.coords[2] for d in line}, {d.coords[0] for d in line}, {d.core_on_chip for d in line}]
    dims = tuple(len(s) for s in spread)
    fits = dims[0] * dims[1] * dims[2] == mesh.shape["row"] and dims[1:] == (2, 2) and dims[0] > 1
    body = make_fast(dims) if fits else body_any
    in_specs = (
        P("slab", "row"),
        P(("slab", "row"), None),
        P(("slab", "row"), None),
        P(("slab", "row"), None),
    )
    out_specs = (P(("slab", "row"), None), P(("slab", "row"), None))
    return jax.shard_map(body, mesh=mesh, in_specs=in_specs, out_specs=out_specs, check_vma=False)
```

```python
import functools
import math

import jax
import jax.numpy as jnp
from jax import lax
from jax.experimental import pallas as pl
from jax.experimental.pallas import tpu as pltpu
from jax.sharding import Mesh, PartitionSpec as P

HB = 32
ITERS = 3
F32 = jnp.float32
BF16 = jnp.bfloat16


SINE = (
    6.283185288846474,
    -16.208955714017648,
    16.769156840921543,
    -9.623969670500662,
    3.5124157106410516,
    -0.7904000717077384,
)


def hadamard_signs(size):
    index = jnp.arange(size, dtype=jnp.int32)
    left = index[:, None]
    right = index[None, :]
    parity = jnp.zeros((size, size), jnp.int32)
    for bit in range(HB.bit_length() - 1):
        parity = parity + jnp.bitwise_and(jnp.right_shift(left, bit), 1) * jnp.bitwise_and(
            jnp.right_shift(right, bit), 1
        )
    signs = jnp.where(parity % 2 == 0, 1.0, -1.0)
    same = (left // HB) == (right // HB)
    return jnp.where(same, signs, 0.0).astype(BF16)


def dot(a, b, dims=((1,), (0,))):
    return lax.dot_general(a, b, (dims, ((), ())), preferred_element_type=F32)


def arrange_kernel(table_ref, *refs):
    *block_refs, high_ref, low_ref = refs
    rows = low_ref.shape[0]
    for i, ref in enumerate(block_refs):
        high_ref[:, i * rows : (i + 1) * rows] = ref[...].astype(BF16)

    @pl.when(pl.program_id(0) == 0)
    def _():
        value = block_refs[0][...]
        low_ref[...] = (value - value.astype(BF16).astype(F32)).astype(BF16)


def arrange(hess_inv, table, group):
    rows = hess_inv.shape[0]
    count = table.shape[0]
    specs = [pl.BlockSpec((rows, rows), lambda i, t, j=j: (0, t[i * group + j])) for j in range(group)]
    return pl.pallas_call(
        arrange_kernel,
        grid_spec=pltpu.PrefetchScalarGridSpec(
            num_scalar_prefetch=1,
            grid=(count // group,),
            in_specs=specs,
            out_specs=[
                pl.BlockSpec((rows, rows * group), lambda i, t: (0, i)),
                pl.BlockSpec((rows, rows), lambda i, t: (0, 0)),
            ],
        ),
        out_shape=[
            jax.ShapeDtypeStruct((rows, rows * count), BF16),
            jax.ShapeDtypeStruct((rows, rows), BF16),
        ],
        name="arrange",
    )(table, *[hess_inv] * group)


def spin(value, signs):
    high = value.astype(BF16)
    low = (value - high.astype(F32)).astype(BF16)
    return dot(signs, high) + dot(signs, low)


def product(hess_refs, piece_refs):
    pieces = list(piece_refs)
    total = None
    for hess_ref in hess_refs:
        at = 0
        while at < hess_ref.shape[1]:
            piece = pieces.pop(0)[...]
            part = dot(hess_ref[:, at : at + piece.shape[0]], piece)
            total = part if total is None else total + part
            at += piece.shape[0]
    return total


def window(hess, first, count):
    rows = hess.shape[0]
    return pl.BlockSpec((rows, rows * count), lambda i: (0, first // count))


def whole(value):
    return pl.BlockSpec(value.shape, lambda i: (0, 0))


def accumulate_kernel(blocks, pieces, *refs):
    total = product(refs[:blocks], refs[blocks : blocks + pieces])
    if len(refs) > blocks + pieces + 1:
        total = total + refs[blocks + pieces][...]
    refs[-1][...] = total


def accumulate(hess, pieces, total=None):
    operands = [h for h, _, _ in hess] + list(pieces) + ([] if total is None else [total])
    rest = operands[len(hess) :]
    return pl.pallas_call(
        functools.partial(accumulate_kernel, len(hess), len(pieces)),
        grid=(1,),
        in_specs=[window(*h) for h in hess] + [whole(v) for v in rest],
        out_specs=whole(pieces[0]),
        out_shape=jax.ShapeDtypeStruct(pieces[0].shape, F32),
        compiler_params=pltpu.CompilerParams(vmem_limit_bytes=32 * 1024 * 1024),
        name="accumulate",
    )(*operands)


def finish_kernel(blocks, pieces, last, *refs):
    total_ref, target_ref, dual_ref, scale_ref, signs_ref, first_ref, second_ref = refs[blocks + pieces :]
    rows, cols = target_ref.shape
    size = signs_ref.shape[0]
    root = F32(1.0 / math.sqrt(HB))
    solved = total_ref[...] + dual_ref[...]
    if pieces:
        solved = solved + product(refs[:blocks], refs[blocks : blocks + pieces])
    for lo in range(0, rows, size):
        span = slice(lo, lo + size)
        total = solved[span]
        spun = spin(total, signs_ref[...]) * root
        share = scale_ref[lo // HB : (lo + size) // HB, :]
        share = jnp.broadcast_to(share[:, None, :], (size // HB, HB, cols)).reshape(size, cols)
        ratio = spun / share
        r = ratio - jnp.round(ratio)
        square = r * r
        series = F32(SINE[-1])
        for term in SINE[-2::-1]:
            series = series * square + F32(term)
        sine = (r - 4.0 * square * r) * series
        snapped = share * (ratio - sine * F32(1.0 / (4.0 * math.pi)))
        fresh = spin(snapped, signs_ref[...]) * root
        dual = total - fresh
        if last:
            first_ref[span, :] = fresh
        else:
            first_ref[span, :] = (target_ref[span, :] + 0.5 * (fresh - dual)).astype(BF16)
        second_ref[span, :] = dual


def finish(hess, pieces, total, target, dual, scale, signs, last):
    rows, cols = target.shape
    operands = [h for h, _, _ in hess] + [*pieces, total, target, dual, scale, signs]
    return pl.pallas_call(
        functools.partial(finish_kernel, len(hess), len(pieces), last),
        grid=(1,),
        in_specs=[window(*h) for h in hess] + [whole(v) for v in operands[len(hess) :]],
        out_specs=[whole(target), whole(target)],
        out_shape=[
            jax.ShapeDtypeStruct((rows, cols), F32 if last else BF16),
            jax.ShapeDtypeStruct((rows, cols), F32),
        ],
        compiler_params=pltpu.CompilerParams(vmem_limit_bytes=32 * 1024 * 1024),
        name="finish_last" if last else "finish",
    )(*operands)


def swap(value, axis):
    return lax.ppermute(value, axis, [(0, 1), (1, 0)])


def arrivals(n, z):
    order = [(0, 0)]
    for s in range(1, n):
        if z - s >= 0:
            order.append((-1, s))
        if z + s < n:
            order.append((1, s))
    return order


def gather_line(own, z, n):
    got = {(0, 0): own}
    up = down = own
    for s in range(1, n):
        up = lax.ppermute(up, "z", [(i, i + 1) for i in range(s - 1, n - 1)])
        down = lax.ppermute(down, "z", [(i, i - 1) for i in range(1, n - s + 1)])
        got[(-1, s)], got[(1, s)] = up, down
    blocks = []
    for q in range(n):
        wanted = {}
        for place in range(n):
            wanted.setdefault(arrivals(n, place)[q], []).append(place)
        value, *others = lax.optimization_barrier([got[key] for key in wanted])
        for other, places in zip(others, list(wanted.values())[1:]):
            here = functools.reduce(jnp.logical_or, [z == p for p in places])
            value = jnp.where(here, other, value)
        blocks.append(value)
    return blocks


def take(value, at, size):
    return lax.dynamic_slice_in_dim(value, at * size, size, 0)


def in_order(first, mine, other):
    low, high = jnp.where(first, mine, other), jnp.where(first, other, mine)
    return jnp.concatenate([low, high], axis=0)


def reduce_tokens(partial, z, x, c):
    size = partial.shape[0] // 2
    mine = take(partial, c, size) + swap(take(partial, 1 - c, size), "core")
    size //= 2
    mine = take(mine, x, size) + swap(take(mine, 1 - x, size), "x")
    low, high = z % 2, z // 2
    pair, cross = [(0, 1), (1, 0), (2, 3), (3, 2)], [(0, 2), (2, 0), (1, 3), (3, 1)]
    size //= 2
    mine = take(mine, low, size) + lax.ppermute(take(mine, 1 - low, size), "z", pair)
    size //= 2
    mine = take(mine, high, size) + lax.ppermute(take(mine, 1 - high, size), "z", cross)
    mine = mine.astype(BF16)
    mine = in_order(high == 0, mine, lax.ppermute(mine, "z", cross))
    mine = in_order(low == 0, mine, lax.ppermute(mine, "z", pair))
    mine = in_order(x == 0, mine, swap(mine, "x"))
    return in_order(c == 0, mine, swap(mine, "core"))


def make_body(dims):
    z_n, x_n, c_n = dims
    every = ("z", "x", "core")

    def body(calib, weights, hess_inv, block_scale):
        rows, cols = weights.shape
        tokens = calib.shape[0]
        z, x, c = (lax.axis_index(a) for a in every)
        signs = hadamard_signs(math.gcd(rows, 256))
        factor = F32(0.25 / math.sqrt(hess_inv.shape[1] * tokens))
        fits = dims == (4, 2, 2)

        partial = dot(calib, weights)
        if fits:
            outputs = reduce_tokens(partial, z, x, c)
        else:
            outputs = lax.psum(partial, every).astype(BF16)

        target_of = lambda outputs: dot(calib, outputs, ((0,), (0,))) * factor
        dual = jnp.zeros((rows, cols), F32)
        if not fits:
            target = target_of(outputs)
            high = lax.reduce_precision(hess_inv, 8, 7)
            low = (hess_inv - high).astype(BF16)
            high = high.astype(BF16)
            right = (target + 0.5 * weights.astype(F32)).astype(BF16)
            for number in range(ITERS):
                right = lax.all_gather(right, every, axis=0, tiled=True)
                total = dot(high, right) + dot(low, right)
                right, dual = finish([], [], total, target, dual, block_scale, signs, number == ITERS - 1)
            return (right, dual)

        order = []
        for q in range(z_n):
            table = [p + d * s for p in range(z_n) for d, s in [arrivals(z_n, p)[q]]]
            zz = jnp.asarray(table, jnp.int32)[z]
            near = [(zz * x_n + x) * c_n + jnp.bitwise_xor(c, co) for co in range(c_n)]
            order.append(near)
        far = [[o + (1 - 2 * x) * c_n for o in near] for near in order]
        order = order[0] + order[1] + far[0] + order[2] + far[1] + order[3] + far[2] + far[3]
        high, low = arrange(hess_inv, jnp.stack(order), 4)
        target = target_of(outputs)
        right = (target + 0.5 * weights.astype(F32)).astype(BF16)

        for number in range(ITERS):
            near = gather_line(right, z, z_n)
            far = []
            for b in near:
                far.append(swap(b, "x"))
            near = [(b, swap(b, "core")) for b in near]
            far = [(b, swap(b, "core")) for b in far]
            total = accumulate([(high, 0, 2), (low, 0, 1)], [*near[0], right])
            total = accumulate([(high, 2, 2), (high, 4, 2)], [*near[1], *far[0]], total)
            total = accumulate([(high, 6, 2), (high, 8, 2)], [*near[2], *far[1]], total)
            total = accumulate([(high, 10, 2), (high, 12, 2)], [*near[3], *far[2]], total)
            right, dual = finish([(high, 14, 2)], far[3], total, target, dual, block_scale, signs, number == ITERS - 1)
        return (right, dual)

    return body


def solution(mesh):
    slabs, rows = mesh.shape["slab"], mesh.shape["row"]
    line = mesh.devices.reshape(slabs, rows)[0]
    spread = [{d.coords[2] for d in line}, {d.coords[0] for d in line}, {d.core_on_chip for d in line}]
    dims = tuple(len(s) for s in spread)
    inner = Mesh(mesh.devices.reshape(slabs, *dims), ("slab", "z", "x", "core"))
    row = ("z", "x", "core")
    rows_spec = P(("slab", *row), None)
    return jax.shard_map(
        make_body(dims),
        mesh=inner,
        in_specs=(P("slab", row), rows_spec, rows_spec, rows_spec),
        out_specs=(rows_spec, rows_spec),
        check_vma=False,
    )
```
